32 devices in a mesh: group: 4 (over y, x), tile: 4 (over z), video: 2 (over core).
Axes of the slice: x: 2, y: 2, z: 4, core: 2. Of those that a mesh axis runs over, the one named last changes fastest.
Arguments:
- features: bfloat16 [8, 8, 16, 24, 384], P(('video', 'tile'), 'group'), parts along dimension 0, may hold values from -6 to 6
- group_slot: int32 [4], replicated, may hold values from 0 to 3, each once
- margins: int32 [4, 4], P('tile'), may hold values from 0 to 4, as said below
- norm_gain: float32 [384], replicated, may hold values from 0.1 to 1.9
- kernel: bfloat16 [3, 3, 3, 384, 384], replicated, may hold values from -0.0625 to 0.0625
- conv_bias: float32 [384], replicated, may hold values from -3 to 3
Outputs:
- decoded: bfloat16 [8, 8, 16, 24, 384], P(('video', 'tile'), 'group'), parts along dimension 0
The draws below stay inside these ranges and needn't reach their ends.
There are 2 independent parts, one for each index of `video`. The reference program is written for one: setup_inputs(seed, part) draws one part's arguments, and reference() takes and returns one part's arrays. A program takes and returns all parts, laid end to end along the dimension named above; an argument that names none is the same for every part. Nothing has to cross between parts.
Inputs may be any that keep to these rules, and one draw needn't show every extreme that they name: group_slot is a permutation of 0 to 3. margins[t] is (left, right, up, down) of tile t; a margin is 0 exactly at the image's border and 1 to 4 elsewhere; the margin a tile has toward a neighbour equals the neighbour's margin back; left and right margins depend only on the tile's column, up and down margins are the same for all columns; some margin equals 4.
All inputs are finite; a program needn't handle non-finite values.
Results may differ from the reference program's by a relative error of at most 0.0043.
Values may be sent and summed in bfloat16 or wider, within the bound.
A program may use at most 128 MiB of HBM per device.

```python
import jax
import jax.numpy as jnp
from jax import lax

C = 384
F = 2
CH = 16
CW = 24
M = 4
GRID_R = 2
FRAMES = 8
N_GROUP = 4
N_TILE = 4


def draw_margins(key, part):
    key_cols, key_rows, key_pick = jax.random.split(key, 3)
    boundaries = N_TILE // GRID_R - 1
    widths = jax.random.randint(key_cols, (boundaries,), 1, M + 1).astype(jnp.int32)
    picked = jax.random.randint(key_pick, (), 0, boundaries)
    widths = jnp.where(jnp.arange(boundaries) == picked, jnp.int32(M), widths)
    height = jax.random.randint(key_rows, (), 1, M + 1).astype(jnp.int32)
    nothing = jnp.zeros((1,), jnp.int32)
    left_cols = jnp.concatenate([nothing, widths])
    right_cols = jnp.concatenate([widths, nothing])
    tile_rows = jnp.arange(N_TILE) // (N_TILE // GRID_R)
    tile_cols = jnp.arange(N_TILE) % (N_TILE // GRID_R)
    left_side = left_cols[tile_cols]
    right_side = right_cols[tile_cols]
    upper = jnp.where(tile_rows > 0, height, 0)
    lower = jnp.where(tile_rows < GRID_R - 1, height, 0)
    return jnp.stack([left_side, right_side, upper, lower], axis=1).astype(jnp.int32)


def block_scale(key, extent, pieces, low, largest):
    def one(dim, parts):
        heights = jax.random.uniform(jax.random.fold_in(jax.random.fold_in(key, 6), dim), (parts,), jnp.float32, low / len(pieces), largest / len(pieces))
        return jnp.repeat(jnp.exp(heights), extent[dim] // parts).reshape((-1,) + (1,) * (len(extent) - dim - 1))

    loudness = one(*pieces[0])
    for cut in pieces[1:]:
        loudness = loudness * one(*cut)
    return loudness


def noise(key, dims, spread, most, cuts=(), kind=jnp.bfloat16):
    gain = block_scale(key, dims, cuts, -0.22, 0.18) if cuts else 1.0
    result = jax.random.normal(key, dims, jnp.float32) * spread * gain
    return jnp.minimum(jnp.maximum(result, -most), most).astype(kind)


def setup_inputs(seed: int = 0, part: int = 0) -> dict:
    streams_of = jax.random.split(jax.random.key(seed), 7)
    part_keys = jax.random.split(jax.random.fold_in(streams_of[6], part), 7)
    return {
        "features": noise(part_keys[0], (N_TILE, FRAMES, CH, CW, C), 1.0, 6.0, ((0, 4), (1, 4))),
        "group_slot": jax.random.permutation(streams_of[1], N_GROUP).astype(jnp.int32),
        "margins": draw_margins(jax.random.fold_in(streams_of[6], 71), part),
        "norm_gain": jnp.clip(1.0 + 0.18 * jax.random.normal(streams_of[3], (C,), jnp.float32), 0.1, 1.9),
        "kernel": noise(streams_of[4], (3, 3, 3, C, C), (27 * C) ** -0.5, 0.0625),
        "conv_bias": noise(streams_of[5], (C,), 0.5, 3.0, (), jnp.float32),
    }


def activate(values, norm_gain):
    widened = values.astype(jnp.float32)
    inv_norm = lax.rsqrt(lax.optimization_barrier(jnp.mean(widened * widened, axis=-1, keepdims=True)) + 1e-06)
    return jax.nn.silu(widened * inv_norm * norm_gain).astype(jnp.bfloat16)

def convolve(padded, kernel, conv_bias, row_count, col_count):
    frame_count = padded.shape[0] - 2
    channels = padded.shape[-1]
    summed = jnp.zeros((frame_count * row_count * col_count, kernel.shape[-1]), jnp.float32)
    for tap_time in range(3):
        for tap_row in range(3):
            window = padded[tap_time:tap_time + frame_count, tap_row:tap_row + row_count]
            stacked = jnp.concatenate([window[:, :, tap_col:tap_col + col_count] for tap_col in range(3)], axis=-1)
            flattened = stacked.reshape(frame_count * row_count * col_count, 3 * channels)
            summed = summed + jnp.dot(flattened, kernel[tap_time, tap_row].reshape(3 * channels, -1), preferred_element_type=jnp.float32)
    return summed.reshape(frame_count, row_count, col_count, -1) + conv_bias

def window_band(step, core, near, far):
    position = jnp.arange(core + 2 * M, dtype=jnp.int32)
    if step == 1:
        return position < M + near
    if step == -1:
        return position >= M + core - far
    return (position >= M - near) & (position < M + core + far)

def rim_weight(step, core, near, far):
    position = jnp.arange(core, dtype=jnp.int32)
    if step == 1:
        distance = position + 1
        margin = near
    elif step == -1:
        distance = core - position
        margin = far
    else:
        return jnp.ones((core,), jnp.float32)
    margin_f = margin.astype(jnp.float32)
    return jnp.maximum(margin_f + 1.0 - distance.astype(jnp.float32), 0.0) / (margin_f + 1.0)

def panel_source(step, core):
    if step == 1:
        return (M + core, M, 0)
    if step == -1:
        return (0, M, core - M)
    return (M, core, 0)

def blend_add(weighted, weight_sum, panel, step_r, step_c, row_dest, col_dest, reaches):
    core_h = weighted.shape[1]
    core_w = weighted.shape[2]
    row_len = panel.shape[1]
    col_len = panel.shape[2]
    placed = jnp.pad(panel.astype(jnp.float32), ((0, 0), (row_dest, core_h - row_dest - row_len), (col_dest, core_w - col_dest - col_len), (0, 0)))
    weight = rim_weight(step_r, core_h, reaches[2], reaches[3])[:, None] * rim_weight(step_c, core_w, reaches[0], reaches[1])[None, :]
    return (weighted + placed * weight[None, :, :, None], weight_sum + weight)

def reference(features, group_slot, margins, norm_gain, kernel, conv_bias):
    tile_count, frames_all, core_h, core_w, channels = features.shape
    grid_cols = tile_count // GRID_R
    by_slot = jnp.argsort(group_slot).astype(jnp.int32)
    blocks = features.reshape(tile_count, N_GROUP, F, core_h, core_w, channels)[:, by_slot]
    timeline = blocks.reshape(GRID_R, grid_cols, frames_all, core_h, core_w, channels)
    timeline = timeline.transpose(2, 0, 3, 1, 4, 5).reshape(frames_all, GRID_R * core_h, grid_cols * core_w, channels)
    activated = jnp.pad(activate(timeline, norm_gain), ((0, 0), (M, M), (M, M), (0, 0)))
    buffer_h = core_h + 2 * M
    buffer_w = core_w + 2 * M

    def tile_conv(tile_index):
        tile_row = (tile_index // grid_cols).astype(jnp.int32)
        tile_col = (tile_index % grid_cols).astype(jnp.int32)
        reaches = margins[tile_index]
        region = lax.dynamic_slice(activated, (jnp.int32(0), tile_row * core_h, tile_col * core_w, jnp.int32(0)), (frames_all, buffer_h, buffer_w, channels))
        inside = window_band(0, core_h, reaches[2], reaches[3])[:, None] & window_band(0, core_w, reaches[0], reaches[1])[None, :]
        region = jnp.where(inside[None, :, :, None], region, jnp.zeros_like(region))
        padded = jnp.pad(region, ((2, 0), (1, 1), (1, 1), (0, 0)))
        return convolve(padded, kernel, conv_bias, buffer_h, buffer_w).astype(jnp.bfloat16)
    tile_outputs = lax.map(tile_conv, jnp.arange(tile_count, dtype=jnp.int32))

    def tile_blend(tile_index):
        reaches = margins[tile_index]
        weighted = jnp.zeros((frames_all, core_h, core_w, channels), jnp.float32)
        weight_sum = jnp.zeros((core_h, core_w), jnp.float32)
        for step_r in (1, 0, -1):
            for step_c in (1, 0, -1):
                source = jnp.clip(tile_index - (step_r * grid_cols + step_c), 0, tile_count - 1)
                outputs = tile_outputs[source]
                row_first, row_len, row_dest = panel_source(step_r, core_h)
                col_first, col_len, col_dest = panel_source(step_c, core_w)
                panel = outputs[:, row_first:row_first + row_len, col_first:col_first + col_len]
                weighted, weight_sum = blend_add(weighted, weight_sum, panel, step_r, step_c, row_dest, col_dest, reaches)
        return (weighted / weight_sum[None, :, :, None]).astype(jnp.bfloat16)
    blended = lax.map(tile_blend, jnp.arange(tile_count, dtype=jnp.int32))
    blended = blended.reshape(tile_count, N_GROUP, F, core_h, core_w, channels)[:, group_slot]
    return blended.reshape(tile_count, frames_all, core_h, core_w, channels)
```

```python
import functools
import itertools

import jax
import jax.numpy as jnp
from jax import lax
from jax.experimental import pallas as pl
from jax.experimental.pallas import tpu as pltpu
from jax.sharding import PartitionSpec as P

GRID_R = 2
MESH = pl.DeviceIdType.MESH
DIRS = ((-1, 0), (1, 0), (0, -1), (0, 1), (-1, -1), (-1, 1), (1, -1), (1, 1))


def activate(values, gain):
    widened = values.astype(jnp.float32)
    inv_norm = lax.rsqrt(jnp.mean(widened * widened, axis=-1, keepdims=True) + 1e-06)
    u = widened * inv_norm * gain
    return u / (1.0 + jnp.exp(-u))


def table(index, values):
    out = jnp.int32(values[0])
    for k in range(1, len(values)):
        out = jnp.where(index == k, jnp.int32(values[k]), out)
    return out


def body(order, n_tile, slot_ref, margin_ref, x_ref, gain_ref, bias_ref, w_hbm, out_ref,
         prev, rows_in, cols_in, corners_in, cols_out, w, act, z, acc,
         send_small, recv_small, send_big, recv_big, w_sem):
    frames, core_h, core_w, channels = x_ref.shape
    n_group = len(order)
    grid_cols = n_tile // GRID_R
    group = lax.axis_index("group")
    tile = lax.axis_index("tile")
    tile_row = tile // grid_cols
    tile_col = tile % grid_cols
    following = [0] * n_group
    preceding = [0] * n_group
    for k in range(n_group):
        following[order[k]] = order[(k + 1) % n_group]
        preceding[order[(k + 1) % n_group]] = order[k]
    nxt = table(group, following)
    before = table(group, preceding)

    for a in (2, 1, 0):
        pltpu.make_async_copy(w_hbm.at[a], w.at[a], w_sem.at[a]).start()

    def present(step_r, step_c):
        ok = None
        for at, step, most in ((tile_row, step_r, GRID_R), (tile_col, step_c, grid_cols)):
            if step == 0:
                continue
            here = (at > 0) if step < 0 else (at < most - 1)
            ok = here if ok is None else jnp.logical_and(ok, here)
        return ok

    barrier = pltpu.get_barrier_semaphore()
    greeted = jnp.int32(2)
    for peer in (nxt, before):
        pl.semaphore_signal(barrier, inc=1, device_id={"group": peer}, device_id_type=MESH)
    for step_r, step_c in DIRS:
        ok = present(step_r, step_c)
        greeted = greeted + 3 * ok.astype(jnp.int32)

        @pl.when(ok)
        def _():
            other = tile + step_r * grid_cols + step_c
            for peer in (group, nxt, before):
                pl.semaphore_signal(barrier, inc=1, device_id={"group": peer, "tile": other},
                                    device_id_type=MESH)

    for f in range(frames):
        edge = x_ref[f].astype(jnp.float32)
        cols_out[0, f] = edge[:, 0, :].astype(jnp.bfloat16)
        cols_out[1, f] = edge[:, core_w - 1, :].astype(jnp.bfloat16)

    pl.semaphore_wait(barrier, greeted)

    def rim_copy(kind, n):
        step_r, step_c = DIRS[n]
        peer = nxt if kind else group
        other = tile + step_r * grid_cols + step_c
        if step_c == 0:
            src = x_ref.at[:, 0 if step_r < 0 else core_h - 1]
            dst = rows_in.at[kind, 1 if step_r < 0 else 0]
        elif step_r == 0:
            src = cols_out.at[0 if step_c < 0 else 1]
            dst = cols_in.at[kind, 1 if step_c < 0 else 0]
        else:
            first = 0 if step_c < 0 else core_w - 8
            src = x_ref.at[:, 0 if step_r < 0 else core_h - 1, pl.ds(first, 8)]
            dst = corners_in.at[kind, 1 if step_r < 0 else 0, 1 if step_c < 0 else 0]
        return pltpu.make_async_remote_copy(
            src_ref=src, dst_ref=dst, send_sem=send_small.at[kind, n], recv_sem=recv_small.at[kind, n],
            device_id={"group": peer, "tile": other}, device_id_type=MESH)

    def block_copy(f):
        return pltpu.make_async_remote_copy(
            src_ref=x_ref.at[f], dst_ref=prev.at[f], send_sem=send_big.at[f], recv_sem=recv_big.at[f],
            device_id={"group": nxt}, device_id_type=MESH)

    for kind in (0, 1):
        for n, (step_r, step_c) in enumerate(DIRS):
            @pl.when(present(step_r, step_c))
            def _():
                rim_copy(kind, n).start()
    for f in (1, 0):
        block_copy(f).start()

    gain = gain_ref[...]
    pitch = core_w + 16
    left, right, up, down = [margin_ref[0, k] for k in range(4)]
    not_first = jnp.full((1, channels), slot_ref[group] > 0)

    def kept(m):
        m_f = jnp.full((core_h, channels), m, jnp.int32).astype(jnp.float32)
        return (m_f + 1.0) / (m_f + 2.0)

    row_at = lax.broadcasted_iota(jnp.int32, (core_h, channels), 0)
    alpha = [jnp.where(row_at == core_h - down, kept(down), 1.0), None,
             jnp.where(row_at == up - 1, kept(up), 1.0)]
    beta_left = kept(left)
    beta_right = kept(right)

    def build(kind, f, source, slot):
        def gated(v):
            return jnp.where(not_first, v, 0.0) if kind else v

        lanes = channels // 128

        def store(at, v):
            for c in range(lanes):
                act[slot, c, at] = v[:, c * 128:(c + 1) * 128]

        def fetch(at):
            return jnp.concatenate([act[slot, c, at] for c in range(lanes)], axis=-1)

        store(pl.ds(0, pitch), jnp.zeros((pitch, channels), jnp.float32))
        store(pl.ds((core_h + 1) * pitch, pitch), jnp.zeros((pitch, channels), jnp.float32))
        store(pl.ds(pitch + 7, core_h, stride=pitch), jnp.zeros((core_h, channels), jnp.float32))
        store(pl.ds(pitch + 8 + core_w, core_h, stride=pitch), jnp.zeros((core_h, channels), jnp.float32))

        def one_row(i, carry):
            at = pl.multiple_of((i + 1) * pitch + 8, 8)
            store(pl.ds(at, core_w), gated(activate(source[f, i], gain)))
            return carry
        lax.fori_loop(0, core_h, one_row, 0, unroll=2)
        for n, (step_r, step_c) in enumerate(DIRS):
            @pl.when(present(step_r, step_c))
            def _():
                vertical = (core_h + 1) * pitch if step_r > 0 else 0
                if step_c == 0:
                    store(pl.ds(vertical + 8, core_w), gated(activate(rows_in[kind, 1 if step_r > 0 else 0, f], gain)))
                elif step_r == 0:
                    start = pitch + (8 + core_w if step_c > 0 else 7)
                    store(pl.ds(start, core_h, stride=pitch),
                          gated(activate(cols_in[kind, 1 if step_c > 0 else 0, f], gain)))
                else:
                    v = gated(activate(corners_in[kind, 1 if step_r > 0 else 0, 1 if step_c > 0 else 0, f], gain))
                    at = vertical + (8 + core_w if step_c > 0 else 7)
                    store(pl.ds(at, 1), v[0:1] if step_c > 0 else v[7:8])

        def one_col(j, carry):
            for b in range(3):
                for e in range(3):
                    v = fetch(pl.ds(b * pitch + 7 + j + e, core_h, stride=pitch))
                    if alpha[b] is not None:
                        v = v * alpha[b]
                    if e == 2:
                        v = jnp.where(j == left - 1, v * beta_left, v)
                    if e == 0:
                        v = jnp.where(j == core_w - right, v * beta_right, v)
                    z[slot, b, pl.ds(pl.multiple_of(j * core_h, core_h), core_h),
                      e * channels:(e + 1) * channels] = v.astype(jnp.bfloat16)
            return carry
        lax.fori_loop(0, core_w, one_col, 0)

    def wait_rims(kind):
        for n, (step_r, step_c) in enumerate(DIRS):
            m = DIRS.index((-step_r, -step_c))

            @pl.when(present(step_r, step_c))
            def _():
                rim_copy(kind, m).wait_recv()

    def wait_w(a):
        pltpu.make_async_copy(w_hbm.at[a], w.at[a], w_sem.at[a]).wait()

    wait_rims(0)
    build(0, 0, x_ref, 0)
    build(0, 1, x_ref, 1)
    wait_w(2)
    wait_w(1)
    acc[...] = jnp.zeros(acc.shape, jnp.float32)

    def both(slot, a_first, a_second):
        def step(b, carry):
            rhs = jnp.concatenate([w[a_first, b], w[a_second, b]], axis=-1)
            acc[...] += jnp.dot(z[slot, b], rhs, preferred_element_type=jnp.float32)
            return carry
        lax.fori_loop(0, 3, step, 0)

    def single(slot, a, s):
        cols = slice(s * channels, (s + 1) * channels)

        def step(b, carry):
            acc[:, cols] += jnp.dot(z[slot, b], w[a, b], preferred_element_type=jnp.float32)
            return carry
        lax.fori_loop(0, 3, step, 0)

    both(0, 2, 1)
    single(1, 2, 1)
    wait_w(0)
    wait_rims(1)
    block_copy(1).wait_recv()
    build(1, 1, prev, 1)
    both(1, 1, 0)
    block_copy(0).wait_recv()
    build(1, 0, prev, 0)
    single(0, 0, 0)

    bias = bias_ref[...]
    for s in range(frames):
        for c in range(channels // 128):
            first = s * channels + c * 128
            act[s, c, pl.ds(0, core_h * core_w)] = acc[:, first:first + 128]

        def put(i, carry):
            v = jnp.concatenate([act[s, c, pl.ds(i, core_w, stride=core_h)] for c in range(channels // 128)], axis=-1)
            out_ref[s, i] = (v + bias).astype(out_ref.dtype)
            return carry
        lax.fori_loop(0, core_h, put, 0)

    for kind in (0, 1):
        for n, (step_r, step_c) in enumerate(DIRS):
            @pl.when(present(step_r, step_c))
            def _():
                rim_copy(kind, n).wait_send()
    for f in (1, 0):
        block_copy(f).wait_send()


def local(orders, n_tile, features, group_slot, margins, norm_gain, kernel, conv_bias):
    x = features[0]
    frames, core_h, core_w, channels = x.shape
    n_group = group_slot.shape[0]
    weights = kernel.reshape(3, 3, 3 * channels, channels)
    rel = lax.rem(group_slot - group_slot[0] + n_group, n_group)
    branch = jnp.int32(0)
    for k, order in enumerate(orders):
        hit = jnp.bool_(True)
        for position, device in enumerate(order):
            hit = hit & (rel[device] == position)
        branch = branch + jnp.where(hit, k, 0)

    pitch = core_w + 16
    vmem = pl.BlockSpec(memory_space=pltpu.VMEM)
    smem = pl.BlockSpec(memory_space=pltpu.SMEM)

    def call(k):
        def run(slot, margin, xx, gain, bias, w):
            return pl.pallas_call(
                functools.partial(body, orders[k], n_tile),
                out_shape=jax.ShapeDtypeStruct(x.shape, jnp.bfloat16),
                in_specs=[smem, smem, vmem, vmem, vmem, pl.BlockSpec(memory_space=pl.ANY)],
                out_specs=vmem,
                scratch_shapes=[
                    pltpu.VMEM((frames, core_h, core_w, channels), jnp.bfloat16),
                    pltpu.VMEM((2, 2, frames, core_w, channels), jnp.bfloat16),
                    pltpu.VMEM((2, 2, frames, core_h, channels), jnp.bfloat16),
                    pltpu.VMEM((2, 2, 2, frames, 8, channels), jnp.bfloat16),
                    pltpu.VMEM((2, frames, core_h, channels), jnp.bfloat16),
                    pltpu.VMEM((3, 3, 3 * channels, channels), jnp.bfloat16),
                    pltpu.VMEM((2, channels // 128, (core_h + 2) * pitch, 128), jnp.float32),
                    pltpu.VMEM((2, 3, core_h * core_w, 3 * channels), jnp.bfloat16),
                    pltpu.VMEM((core_h * core_w, 2 * channels), jnp.float32),
                    pltpu.SemaphoreType.DMA((2, 8)),
                    pltpu.SemaphoreType.DMA((2, 8)),
                    pltpu.SemaphoreType.DMA((2,)),
                    pltpu.SemaphoreType.DMA((2,)),
                    pltpu.SemaphoreType.DMA((3,)),
                ],
                compiler_params=pltpu.CompilerParams(collective_id=k, has_side_effects=True),
                name="conv_order_%d" % k,
            )(slot, margin, xx, gain, bias, w)
        return run

    out = lax.switch(branch, [call(k) for k in range(len(orders))], group_slot, margins, x,
                     norm_gain[None], conv_bias[None], weights)
    return out[None]


def solution(mesh):
    n_group = mesh.shape["group"]
    n_tile = mesh.shape["tile"]
    orders = [(0,) + rest for rest in itertools.permutations(range(1, n_group))]
    return jax.shard_map(
        functools.partial(local, orders, n_tile),
        mesh=mesh,
        in_specs=(
            P(("video", "tile"), "group", None, None, None),
            P(),
            P("tile", None),
            P(),
            P(),
            P(),
        ),
        out_specs=P(("video", "tile"), "group", None, None, None),
        check_vma=False,
    )
```

```python
import functools
import itertools

import jax
import jax.numpy as jnp
from jax import lax
from jax.experimental import pallas as pl
from jax.experimental.pallas import tpu as pltpu
from jax.sharding import PartitionSpec as P

GRID_R = 2
MESH = pl.DeviceIdType.MESH
DIRS = ((-1, 0), (1, 0), (0, -1), (0, 1), (-1, -1), (-1, 1), (1, -1), (1, 1))


def activate(values, gain):
    widened = values.astype(jnp.float32)
    inv_norm = lax.rsqrt(jnp.mean(widened * widened, axis=-1, keepdims=True) + 1e-06)
    half = widened * inv_norm * (0.5 * gain)
    return half + half * jnp.tanh(half)


def table(index, values):
    out = jnp.int32(values[0])
    for k in range(1, len(values)):
        out = jnp.where(index == k, jnp.int32(values[k]), out)
    return out


def body(order, n_tile, slot_ref, margin_ref, x_ref, gain_ref, bias_ref, w_hbm, out_ref,
         prev, rows_in, cols_in, corners_in, cols_out, w, act, z, acc,
         send_small, recv_small, send_big, recv_big, w_sem):
    frames, core_h, core_w, channels = x_ref.shape
    n_group = len(order)
    grid_cols = n_tile // GRID_R
    group = lax.axis_index("group")
    tile = lax.axis_index("tile")
    tile_row = tile // grid_cols
    tile_col = tile % grid_cols
    following = [0] * n_group
    preceding = [0] * n_group
    for k in range(n_group):
        following[order[k]] = order[(k + 1) % n_group]
        preceding[order[(k + 1) % n_group]] = order[k]
    nxt = table(group, following)
    before = table(group, preceding)

    for a in (2, 1, 0):
        pltpu.make_async_copy(w_hbm.at[a], w.at[a], w_sem.at[a]).start()

    def present(step_r, step_c):
        ok = None
        for at, step, most in ((tile_row, step_r, GRID_R), (tile_col, step_c, grid_cols)):
            if step == 0:
                continue
            here = (at > 0) if step < 0 else (at < most - 1)
            ok = here if ok is None else jnp.logical_and(ok, here)
        return ok

    barrier = pltpu.get_barrier_semaphore()
    greeted = jnp.int32(2)
    for peer in (nxt, before):
        pl.semaphore_signal(barrier, inc=1, device_id={"group": peer}, device_id_type=MESH)
    for step_r, step_c in DIRS:
        ok = present(step_r, step_c)
        greeted = greeted + 3 * ok.astype(jnp.int32)

        @pl.when(ok)
        def _():
            other = tile + step_r * grid_cols + step_c
            for peer in (group, nxt, before):
                pl.semaphore_signal(barrier, inc=1, device_id={"group": peer, "tile": other},
                                    device_id_type=MESH)

    for f in range(frames):
        edge = x_ref[f].astype(jnp.float32)
        cols_out[0, f] = edge[:, 0, :].astype(jnp.bfloat16)
        cols_out[1, f] = edge[:, core_w - 1, :].astype(jnp.bfloat16)

    pl.semaphore_wait(barrier, greeted)

    def rim_copy(kind, n):
        step_r, step_c = DIRS[n]
        peer = nxt if kind else group
        other = tile + step_r * grid_cols + step_c
        if step_c == 0:
            src = x_ref.at[:, 0 if step_r < 0 else core_h - 1]
            dst = rows_in.at[kind, 1 if step_r < 0 else 0]
        elif step_r == 0:
            src = cols_out.at[0 if step_c < 0 else 1]
            dst = cols_in.at[kind, 1 if step_c < 0 else 0]
        else:
            first = 0 if step_c < 0 else core_w - 8
            src = x_ref.at[:, 0 if step_r < 0 else core_h - 1, pl.ds(first, 8)]
            dst = corners_in.at[kind, 1 if step_r < 0 else 0, 1 if step_c < 0 else 0]
        return pltpu.make_async_remote_copy(
            src_ref=src, dst_ref=dst, send_sem=send_small.at[kind, n], recv_sem=recv_small.at[kind, n],
            device_id={"group": peer, "tile": other}, device_id_type=MESH)

    def block_copy(f):
        return pltpu.make_async_remote_copy(
            src_ref=x_ref.at[f], dst_ref=prev.at[f], send_sem=send_big.at[f], recv_sem=recv_big.at[f],
            device_id={"group": nxt}, device_id_type=MESH)

    for kind in (0, 1):
        for n, (step_r, step_c) in enumerate(DIRS):
            @pl.when(present(step_r, step_c))
            def _():
                rim_copy(kind, n).start()
    for f in (1, 0):
        block_copy(f).start()

    gain = gain_ref[...].reshape(1, channels)
    pitch = core_w + 16
    left, right, up, down = [margin_ref[0, k] for k in range(4)]
    not_first = jnp.full((1, channels), slot_ref[group] > 0)

    def kept(m):
        m_f = jnp.full((core_h, channels), m, jnp.int32).astype(jnp.float32)
        return (m_f + 1.0) / (m_f + 2.0)

    row_at = lax.broadcasted_iota(jnp.int32, (core_h, channels), 0)
    alpha = [jnp.where(row_at == core_h - down, kept(down), 1.0), None,
             jnp.where(row_at == up - 1, kept(up), 1.0)]
    beta_left = kept(left)
    beta_right = kept(right)

    def build(kind, f, source, slot):
        def gated(v):
            return jnp.where(not_first, v, 0.0) if kind else v

        lanes = channels // 128

        def store(at, v):
            for c in range(lanes):
                act[slot, c, at] = v[:, c * 128:(c + 1) * 128]

        def fetch(at):
            return jnp.concatenate([act[slot, c, at] for c in range(lanes)], axis=-1)

        store(pl.ds(0, pitch), jnp.zeros((pitch, channels), jnp.float32))
        store(pl.ds((core_h + 1) * pitch, pitch), jnp.zeros((pitch, channels), jnp.float32))
        store(pl.ds(pitch + 7, core_h, stride=pitch), jnp.zeros((core_h, channels), jnp.float32))
        store(pl.ds(pitch + 8 + core_w, core_h, stride=pitch), jnp.zeros((core_h, channels), jnp.float32))

        def one_row(i, carry):
            for k in range(4):
                at = pl.multiple_of((4 * i + k + 1) * pitch + 8, 8)
                store(pl.ds(at, core_w), gated(activate(source[f, 4 * i + k], gain)))
            return carry
        lax.fori_loop(0, core_h // 4, one_row, 0)
        for n, (step_r, step_c) in enumerate(DIRS):
            @pl.when(present(step_r, step_c))
            def _():
                vertical = (core_h + 1) * pitch if step_r > 0 else 0
                if step_c == 0:
                    store(pl.ds(vertical + 8, core_w), gated(activate(rows_in[kind, 1 if step_r > 0 else 0, f], gain)))
                elif step_r == 0:
                    start = pitch + (8 + core_w if step_c > 0 else 7)
                    store(pl.ds(start, core_h, stride=pitch),
                          gated(activate(cols_in[kind, 1 if step_c > 0 else 0, f], gain)))
                else:
                    v = gated(activate(corners_in[kind, 1 if step_r > 0 else 0, 1 if step_c > 0 else 0, f], gain))
                    at = vertical + (8 + core_w if step_c > 0 else 7)
                    store(pl.ds(at, 1), v[0:1] if step_c > 0 else v[7:8])

        def one_col(j, carry):
            for b in range(3):
                for e in range(3):
                    v = fetch(pl.ds(b * pitch + 7 + j + e, core_h, stride=pitch))
                    if alpha[b] is not None:
                        v = v * alpha[b]
                    if e == 2:
                        v = jnp.where(j == left - 1, v * beta_left, v)
                    if e == 0:
                        v = jnp.where(j == core_w - right, v * beta_right, v)
                    z[slot, b, pl.ds(pl.multiple_of(j * core_h, core_h), core_h),
                      e * channels:(e + 1) * channels] = v.astype(jnp.bfloat16)
            return carry
        lax.fori_loop(0, core_w, one_col, 0, unroll=2)

    def wait_rims(kind):
        for n, (step_r, step_c) in enumerate(DIRS):
            m = DIRS.index((-step_r, -step_c))

            @pl.when(present(step_r, step_c))
            def _():
                rim_copy(kind, m).wait_recv()

    def wait_w(a):
        pltpu.make_async_copy(w_hbm.at[a], w.at[a], w_sem.at[a]).wait()

    wait_rims(0)
    build(0, 0, x_ref, 0)
    build(0, 1, x_ref, 1)
    wait_w(2)
    wait_w(1)
    acc[...] = jnp.zeros(acc.shape, jnp.float32)

    def both(slot, a_first, a_second):
        def step(b, carry):
            rhs = jnp.concatenate([w[a_first, b], w[a_second, b]], axis=-1)
            acc[...] += jnp.dot(z[slot, b], rhs, preferred_element_type=jnp.float32)
            return carry
        lax.fori_loop(0, 3, step, 0)

    def single(slot, a, s):
        cols = slice(s * channels, (s + 1) * channels)

        def step(b, carry):
            acc[:, cols] += jnp.dot(z[slot, b], w[a, b], preferred_element_type=jnp.float32)
            return carry
        lax.fori_loop(0, 3, step, 0)

    both(0, 2, 1)
    single(1, 2, 1)
    wait_w(0)
    wait_rims(1)
    block_copy(1).wait_recv()
    build(1, 1, prev, 1)
    both(1, 1, 0)
    block_copy(0).wait_recv()
    build(1, 0, prev, 0)
    single(0, 0, 0)

    bias = bias_ref[...].reshape(1, channels)
    for s in range(frames):
        for c in range(channels // 128):
            first = s * channels + c * 128
            act[s, c, pl.ds(0, core_h * core_w)] = acc[:, first:first + 128]

        def put(i, carry):
            v = jnp.concatenate([act[s, c, pl.ds(i, core_w, stride=core_h)] for c in range(channels // 128)], axis=-1)
            out_ref[s, i] = (v + bias).astype(out_ref.dtype)
            return carry
        lax.fori_loop(0, core_h, put, 0)

    for kind in (0, 1):
        for n, (step_r, step_c) in enumerate(DIRS):
            @pl.when(present(step_r, step_c))
            def _():
                rim_copy(kind, n).wait_send()
    for f in (1, 0):
        block_copy(f).wait_send()


def pick(orders, slot_ref, branch_ref):
    n_group = len(orders[0])
    rel = [lax.rem(slot_ref[d] - slot_ref[0] + n_group, n_group) for d in range(n_group)]
    branch = jnp.int32(0)
    for k, order in enumerate(orders):
        hit = jnp.bool_(True)
        for position, device in enumerate(order):
            hit = jnp.logical_and(hit, rel[device] == position)
        branch = jnp.where(hit, jnp.int32(k), branch)
    branch_ref[0] = branch


def local(orders, n_tile, features, group_slot, margins, norm_gain, kernel, conv_bias):
    x = features[0]
    frames, core_h, core_w, channels = x.shape
    weights = kernel.reshape(3, 3, 3 * channels, channels)
    branch = pl.pallas_call(
        functools.partial(pick, orders),
        out_shape=jax.ShapeDtypeStruct((1,), jnp.int32),
        in_specs=[pl.BlockSpec(memory_space=pltpu.SMEM)],
        out_specs=pl.BlockSpec(memory_space=pltpu.SMEM),
        name="pick",
    )(group_slot)[0]

    pitch = core_w + 16
    vmem = pl.BlockSpec(memory_space=pltpu.VMEM)
    smem = pl.BlockSpec(memory_space=pltpu.SMEM)

    def call(k):
        def run(slot, margin, xx, gain, bias, w):
            return pl.pallas_call(
                functools.partial(body, orders[k], n_tile),
                out_shape=jax.ShapeDtypeStruct(x.shape, jnp.bfloat16),
                in_specs=[smem, smem, vmem, vmem, vmem, pl.BlockSpec(memory_space=pl.ANY)],
                out_specs=vmem,
                scratch_shapes=[
                    pltpu.VMEM((frames, core_h, core_w, channels), jnp.bfloat16),
                    pltpu.VMEM((2, 2, frames, core_w, channels), jnp.bfloat16),
                    pltpu.VMEM((2, 2, frames, core_h, channels), jnp.bfloat16),
                    pltpu.VMEM((2, 2, 2, frames, 8, channels), jnp.bfloat16),
                    pltpu.VMEM((2, frames, core_h, channels), jnp.bfloat16),
                    pltpu.VMEM((3, 3, 3 * channels, channels), jnp.bfloat16),
                    pltpu.VMEM((2, channels // 128, (core_h + 2) * pitch, 128), jnp.float32),
                    pltpu.VMEM((2, 3, core_h * core_w, 3 * channels), jnp.bfloat16),
                    pltpu.VMEM((core_h * core_w, 2 * channels), jnp.float32),
                    pltpu.SemaphoreType.DMA((2, 8)),
                    pltpu.SemaphoreType.DMA((2, 8)),
                    pltpu.SemaphoreType.DMA((2,)),
                    pltpu.SemaphoreType.DMA((2,)),
                    pltpu.SemaphoreType.DMA((3,)),
                ],
                compiler_params=pltpu.CompilerParams(collective_id=k, has_side_effects=True),
                name="conv_order_%d" % k,
            )(slot, margin, xx, gain, bias, w)
        return run

    out = lax.switch(branch, [call(k) for k in range(len(orders))], group_slot, margins, x,
                     norm_gain, conv_bias, weights)
    return out[None]


def solution(mesh):
    n_group = mesh.shape["group"]
    n_tile = mesh.shape["tile"]
    orders = [(0,) + rest for rest in itertools.permutations(range(1, n_group))]
    return jax.shard_map(
        functools.partial(local, orders, n_tile),
        mesh=mesh,
        in_specs=(
            P(("video", "tile"), "group", None, None, None),
            P(),
            P("tile", None),
            P(),
            P(),
            P(),
        ),
        out_specs=P(("video", "tile"), "group", None, None, None),
        check_vma=False,
    )
```

```python
import functools
import itertools

import jax
import jax.numpy as jnp
from jax import lax
from jax.experimental import pallas as pl
from jax.experimental.pallas import tpu as pltpu
from jax.sharding import PartitionSpec as P

GRID_R = 2
MESH = pl.DeviceIdType.MESH
DIRS = ((-1, 0), (1, 0), (0, -1), (0, 1), (-1, -1), (-1, 1), (1, -1), (1, 1))


def activate(values, gain):
    widened = values.astype(jnp.float32)
    inv_norm = lax.rsqrt(jnp.mean(widened * widened, axis=-1, keepdims=True) + 1e-06)
    half = widened * inv_norm * (0.5 * gain)
    return half + half * jnp.tanh(half)


def table(index, values):
    out = jnp.int32(values[0])
    for k in range(1, len(values)):
        out = jnp.where(index == k, jnp.int32(values[k]), out)
    return out


def body(order, n_tile, slot_ref, margin_ref, x_hbm, gain_ref, bias_ref, w_hbm, out_ref,
         x_ref, prev, rows_in, cols_in, corners_in, cols_out, w, act, z, acc,
         send_small, recv_small, send_big, recv_big, w_sem, x_sem):
    frames, core_h, core_w, channels = x_ref.shape
    n_group = len(order)
    grid_cols = n_tile // GRID_R
    group = lax.axis_index("group")
    tile = lax.axis_index("tile")
    tile_row = tile // grid_cols
    tile_col = tile % grid_cols
    following = [0] * n_group
    preceding = [0] * n_group
    for k in range(n_group):
        following[order[k]] = order[(k + 1) % n_group]
        preceding[order[(k + 1) % n_group]] = order[k]
    nxt = table(group, following)
    before = table(group, preceding)

    x_copy = pltpu.make_async_copy(x_hbm, x_ref, x_sem)
    x_copy.start()
    for a in (2, 1, 0):
        pltpu.make_async_copy(w_hbm.at[a], w.at[a], w_sem.at[a]).start()

    def present(step_r, step_c):
        ok = None
        for at, step, most in ((tile_row, step_r, GRID_R), (tile_col, step_c, grid_cols)):
            if step == 0:
                continue
            here = (at > 0) if step < 0 else (at < most - 1)
            ok = here if ok is None else jnp.logical_and(ok, here)
        return ok

    barrier = pltpu.get_barrier_semaphore()
    greeted = jnp.int32(2)
    for peer in (nxt, before):
        pl.semaphore_signal(barrier, inc=1, device_id={"group": peer}, device_id_type=MESH)
    for step_r, step_c in DIRS:
        ok = present(step_r, step_c)
        greeted = greeted + 3 * ok.astype(jnp.int32)

        @pl.when(ok)
        def _():
            other = tile + step_r * grid_cols + step_c
            for peer in (group, nxt, before):
                pl.semaphore_signal(barrier, inc=1, device_id={"group": peer, "tile": other},
                                    device_id_type=MESH)

    x_copy.wait()
    for f in range(frames):
        edge = x_ref[f].astype(jnp.float32)
        cols_out[0, f] = edge[:, 0, :].astype(jnp.bfloat16)
        cols_out[1, f] = edge[:, core_w - 1, :].astype(jnp.bfloat16)

    pl.semaphore_wait(barrier, greeted)

    def rim_copy(kind, n):
        step_r, step_c = DIRS[n]
        peer = nxt if kind else group
        other = tile + step_r * grid_cols + step_c
        if step_c == 0:
            src = x_ref.at[:, 0 if step_r < 0 else core_h - 1]
            dst = rows_in.at[kind, 1 if step_r < 0 else 0]
        elif step_r == 0:
            src = cols_out.at[0 if step_c < 0 else 1]
            dst = cols_in.at[kind, 1 if step_c < 0 else 0]
        else:
            first = 0 if step_c < 0 else core_w - 8
            src = x_ref.at[:, 0 if step_r < 0 else core_h - 1, pl.ds(first, 8)]
            dst = corners_in.at[kind, 1 if step_r < 0 else 0, 1 if step_c < 0 else 0]
        return pltpu.make_async_remote_copy(
            src_ref=src, dst_ref=dst, send_sem=send_small.at[kind, n], recv_sem=recv_small.at[kind, n],
            device_id={"group": peer, "tile": other}, device_id_type=MESH)

    def block_copy(f):
        return pltpu.make_async_remote_copy(
            src_ref=x_ref.at[f], dst_ref=prev.at[f], send_sem=send_big.at[f], recv_sem=recv_big.at[f],
            device_id={"group": nxt}, device_id_type=MESH)

    for kind in (0, 1):
        for n, (step_r, step_c) in enumerate(DIRS):
            @pl.when(present(step_r, step_c))
            def _():
                rim_copy(kind, n).start()
    for f in (1, 0):
        block_copy(f).start()

    gain = gain_ref[...].reshape(1, channels)
    pitch = core_w + 16
    left, right, up, down = [margin_ref[0, k] for k in range(4)]
    not_first = jnp.full((1, channels), slot_ref[group] > 0)

    def kept(m):
        m_f = jnp.full((core_h, channels), m, jnp.int32).astype(jnp.float32)
        return (m_f + 1.0) / (m_f + 2.0)

    row_at = lax.broadcasted_iota(jnp.int32, (core_h, channels), 0)
    alpha = [jnp.where(row_at == core_h - down, kept(down), 1.0), None,
             jnp.where(row_at == up - 1, kept(up), 1.0)]
    beta_left = kept(left)
    beta_right = kept(right)

    lanes = channels // 128

    def gate(kind, v):
        return jnp.where(not_first, v, 0.0) if kind else v

    def put_act(slot, at, v):
        for c in range(lanes):
            act[slot, c, at] = v[:, c * 128:(c + 1) * 128]

    def interior(kind, f, source, slot):
        gated = functools.partial(gate, kind)
        store = functools.partial(put_act, slot)

        store(pl.ds(0, pitch), jnp.zeros((pitch, channels), jnp.float32))
        store(pl.ds((core_h + 1) * pitch, pitch), jnp.zeros((pitch, channels), jnp.float32))
        store(pl.ds(pitch + 7, core_h, stride=pitch), jnp.zeros((core_h, channels), jnp.float32))
        store(pl.ds(pitch + 8 + core_w, core_h, stride=pitch), jnp.zeros((core_h, channels), jnp.float32))

        def one_row(i, carry):
            for k in range(4):
                at = pl.multiple_of((4 * i + k + 1) * pitch + 8, 8)
                store(pl.ds(at, core_w), gated(activate(source[f, 4 * i + k], gain)))
            return carry
        lax.fori_loop(0, core_h // 4, one_row, 0)

    def finish(kind, f, slot):
        gated = functools.partial(gate, kind)
        store = functools.partial(put_act, slot)

        def fetch(at):
            return jnp.concatenate([act[slot, c, at] for c in range(lanes)], axis=-1)

        for n, (step_r, step_c) in enumerate(DIRS):
            @pl.when(present(step_r, step_c))
            def _():
                vertical = (core_h + 1) * pitch if step_r > 0 else 0
                if step_c == 0:
                    store(pl.ds(vertical + 8, core_w), gated(activate(rows_in[kind, 1 if step_r > 0 else 0, f], gain)))
                elif step_r == 0:
                    start = pitch + (8 + core_w if step_c > 0 else 7)
                    store(pl.ds(start, core_h, stride=pitch),
                          gated(activate(cols_in[kind, 1 if step_c > 0 else 0, f], gain)))
                else:
                    v = gated(activate(corners_in[kind, 1 if step_r > 0 else 0, 1 if step_c > 0 else 0, f], gain))
                    at = vertical + (8 + core_w if step_c > 0 else 7)
                    store(pl.ds(at, 1), v[0:1] if step_c > 0 else v[7:8])

        def one_col(j, carry):
            for b in range(3):
                for e in range(3):
                    v = fetch(pl.ds(b * pitch + 7 + j + e, core_h, stride=pitch))
                    if alpha[b] is not None:
                        v = v * alpha[b]
                    if e == 2:
                        v = jnp.where(j == left - 1, v * beta_left, v)
                    if e == 0:
                        v = jnp.where(j == core_w - right, v * beta_right, v)
                    z[slot, b, pl.ds(pl.multiple_of(j * core_h, core_h), core_h),
                      e * channels:(e + 1) * channels] = v.astype(jnp.bfloat16)
            return carry
        lax.fori_loop(0, core_w, one_col, 0, unroll=2)

    def wait_rims(kind):
        for n, (step_r, step_c) in enumerate(DIRS):
            m = DIRS.index((-step_r, -step_c))

            @pl.when(present(step_r, step_c))
            def _():
                rim_copy(kind, m).wait_recv()

    def wait_w(a):
        pltpu.make_async_copy(w_hbm.at[a], w.at[a], w_sem.at[a]).wait()

    interior(0, 0, x_ref, 0)
    interior(0, 1, x_ref, 1)
    wait_rims(0)
    finish(0, 0, 0)
    finish(0, 1, 1)
    wait_w(2)
    wait_w(1)
    acc[...] = jnp.zeros(acc.shape, jnp.float32)

    def both(slot, a_first, a_second):
        def step(b, carry):
            rhs = jnp.concatenate([w[a_first, b], w[a_second, b]], axis=-1)
            acc[...] += jnp.dot(z[slot, b], rhs, preferred_element_type=jnp.float32)
            return carry
        lax.fori_loop(0, 3, step, 0)

    def single(slot, a, s):
        cols = slice(s * channels, (s + 1) * channels)

        def step(b, carry):
            acc[:, cols] += jnp.dot(z[slot, b], w[a, b], preferred_element_type=jnp.float32)
            return carry
        lax.fori_loop(0, 3, step, 0)

    both(0, 2, 1)
    single(1, 2, 1)
    wait_w(0)
    wait_rims(1)
    block_copy(1).wait_recv()
    interior(1, 1, prev, 1)
    finish(1, 1, 1)
    both(1, 1, 0)
    bias = bias_ref[...].reshape(1, channels)

    def give(s):
        for c in range(lanes):
            first = s * channels + c * 128
            act[s, c, pl.ds(0, core_h * core_w)] = acc[:, first:first + 128]

        def put(i, carry):
            v = jnp.concatenate([act[s, c, pl.ds(i, core_w, stride=core_h)] for c in range(lanes)], axis=-1)
            out_ref[s, i] = (v + bias).astype(out_ref.dtype)
            return carry
        lax.fori_loop(0, core_h, put, 0, unroll=4)

    give(1)
    block_copy(0).wait_recv()
    interior(1, 0, prev, 0)
    finish(1, 0, 0)
    single(0, 0, 0)
    give(0)

    for kind in (0, 1):
        for n, (step_r, step_c) in enumerate(DIRS):
            @pl.when(present(step_r, step_c))
            def _():
                rim_copy(kind, n).wait_send()
    for f in (1, 0):
        block_copy(f).wait_send()


def pick(orders, slot_ref, branch_ref):
    n_group = len(orders[0])
    rel = [lax.rem(slot_ref[d] - slot_ref[0] + n_group, n_group) for d in range(n_group)]
    branch = jnp.int32(0)
    for k, order in enumerate(orders):
        hit = jnp.bool_(True)
        for position, device in enumerate(order):
            hit = jnp.logical_and(hit, rel[device] == position)
        branch = jnp.where(hit, jnp.int32(k), branch)
    branch_ref[0] = branch


def local(orders, n_tile, features, group_slot, margins, norm_gain, kernel, conv_bias):
    x = features[0]
    frames, core_h, core_w, channels = x.shape
    weights = kernel.reshape(3, 3, 3 * channels, channels)
    branch = pl.pallas_call(
        functools.partial(pick, orders),
        out_shape=jax.ShapeDtypeStruct((1,), jnp.int32),
        in_specs=[pl.BlockSpec(memory_space=pltpu.SMEM)],
        out_specs=pl.BlockSpec(memory_space=pltpu.SMEM),
        name="pick",
    )(group_slot)[0]

    pitch = core_w + 16
    vmem = pl.BlockSpec(memory_space=pltpu.VMEM)
    smem = pl.BlockSpec(memory_space=pltpu.SMEM)

    def call(k):
        def run(slot, margin, xx, gain, bias, w):
            return pl.pallas_call(
                functools.partial(body, orders[k], n_tile),
                out_shape=jax.ShapeDtypeStruct(x.shape, jnp.bfloat16),
                in_specs=[smem, smem, pl.BlockSpec(memory_space=pl.ANY), vmem, vmem, pl.BlockSpec(memory_space=pl.ANY)],
                out_specs=vmem,
                scratch_shapes=[
                    pltpu.VMEM((frames, core_h, core_w, channels), jnp.bfloat16),
                    pltpu.VMEM((frames, core_h, core_w, channels), jnp.bfloat16),
                    pltpu.VMEM((2, 2, frames, core_w, channels), jnp.bfloat16),
                    pltpu.VMEM((2, 2, frames, core_h, channels), jnp.bfloat16),
                    pltpu.VMEM((2, 2, 2, frames, 8, channels), jnp.bfloat16),
                    pltpu.VMEM((2, frames, core_h, channels), jnp.bfloat16),
                    pltpu.VMEM((3, 3, 3 * channels, channels), jnp.bfloat16),
                    pltpu.VMEM((2, channels // 128, (core_h + 2) * pitch, 128), jnp.float32),
                    pltpu.VMEM((2, 3, core_h * core_w, 3 * channels), jnp.bfloat16),
                    pltpu.VMEM((core_h * core_w, 2 * channels), jnp.float32),
                    pltpu.SemaphoreType.DMA((2, 8)),
                    pltpu.SemaphoreType.DMA((2, 8)),
                    pltpu.SemaphoreType.DMA((2,)),
                    pltpu.SemaphoreType.DMA((2,)),
                    pltpu.SemaphoreType.DMA((3,)),
                    pltpu.SemaphoreType.DMA,
                ],
                compiler_params=pltpu.CompilerParams(collective_id=k, has_side_effects=True),
                name="conv_order_%d" % k,
            )(slot, margin, xx, gain, bias, w)
        return run

    out = lax.switch(branch, [call(k) for k in range(len(orders))], group_slot, margins, x,
                     norm_gain, conv_bias, weights)
    return out[None]


def solution(mesh):
    n_group = mesh.shape["group"]
    n_tile = mesh.shape["tile"]
    orders = [(0,) + rest for rest in itertools.permutations(range(1, n_group))]
    return jax.shard_map(
        functools.partial(local, orders, n_tile),
        mesh=mesh,
        in_specs=(
            P(("video", "tile"), "group", None, None, None),
            P(),
            P("tile", None),
            P(),
            P(),
            P(),
        ),
        out_specs=P(("video", "tile"), "group", None, None, None),
        check_vma=False,
    )
```
